32 devices in a mesh: slab: 2 (over x), scan: 8 (over z, y), mz: 2 (over core).
Axes of the slice: x: 2, y: 2, z: 4, core: 2. Of those that a mesh axis runs over, the one named last changes fastest.
Arguments:
- spectra: bfloat16 [12288, 8192], P('mz', ('slab', 'scan')), parts along dimension 1, may hold values from 0 to 1
- templates: bfloat16 [2, 12288, 512], P('mz', ('slab', 'scan')), parts along dimension 1, may hold values from 0 to 2
- activations: float32 [64, 8192], P(None, ('slab', 'scan')), parts along dimension 1, may hold values from 0 to 1
- h_rate: float32 [64], replicated, may hold values from 0.02 to 0.08
- w_rate: float32 [64], replicated, may hold values from 0.2 to 0.8
Outputs:
- new_activations: float32 [64, 8192], P(None, ('slab', 'scan')), parts along dimension 1
- new_templates: bfloat16 [2, 12288, 512], P('mz', ('slab', 'scan')), parts along dimension 1
The draws below stay inside these ranges and needn't reach their ends.
There are 2 independent parts, one for each index of `slab`. The reference program is written for one: setup_inputs(seed, part) draws one part's arguments, and reference() takes and returns one part's arrays. A program takes and returns all parts, laid end to end along the dimension named above; an argument that names none is the same for every part. Nothing has to cross between parts.
All inputs are finite; a program needn't handle non-finite values.
Results may differ from the reference program's by a relative error of at most 0.00082.
Values may be sent and summed in bfloat16 or wider, within the bound.
No kernel may reach another device: no remote copies, remote signals or barrier semaphores. Data moves between devices by JAX's collectives and lax.ppermute only.
A program may use at most 128 MiB of HBM per device.

```python
import math
import jax
import jax.numpy as jnp
from jax import lax

M = 12288
K = 64
LAGS = 8
LAG = 64
SCAN_DEV = 512
SPAN = 448
SCANS = 4096
N_SCAN = 8
N_MZ = 2


def unit_values(key, shape):
    return jax.random.uniform(key, shape, jnp.float32, 0.0, 1.0)


def draw_spectra(key, part):
    inner = jax.random.fold_in(key, 11)
    return unit_values(inner, (M, SCAN_DEV * N_SCAN)).astype(jnp.bfloat16)


def draw_templates(key, part):
    inner = jax.random.fold_in(key, 23)
    return (2.0 * unit_values(inner, (N_MZ, M // N_MZ, LAGS * K))).astype(jnp.bfloat16)


def draw_activations(key, part):
    inner = jax.random.fold_in(key, 37)
    return unit_values(inner, (K, SCAN_DEV * N_SCAN)).astype(jnp.float32)


def setup_inputs(seed: int = 0, part: int = 0) -> dict:
    key_of = jax.random.split(jax.random.key(seed), 6)
    part_splits = jax.random.split(jax.random.fold_in(key_of[5], part), 6)
    spectra = draw_spectra(jax.random.fold_in(jax.random.fold_in(key_of[5], part), 71), part)
    templates = draw_templates(jax.random.fold_in(jax.random.fold_in(key_of[5], part), 71), part)
    activations = draw_activations(jax.random.fold_in(jax.random.fold_in(key_of[5], part), 71), part)
    h_rate = jnp.clip(jnp.exp(jax.random.uniform(key_of[3], (K,), jnp.float32, math.log(0.02), math.log(0.08))), 0.02, 0.08)
    w_rate = jnp.clip(jnp.exp(jax.random.uniform(key_of[4], (K,), jnp.float32, math.log(0.2), math.log(0.8))), 0.2, 0.8)
    return {"spectra": spectra, "templates": templates, "activations": activations, "h_rate": h_rate, "w_rate": w_rate}


def lagged(hb):
    padded = jnp.pad(hb, ((0, 0), (SPAN, 0)))
    return jnp.concatenate([padded[:, SPAN - l * LAG:SPAN - l * LAG + SCANS] for l in range(LAGS)], 0)


def product(a, b):
    return jnp.dot(a.astype(jnp.float32), b.astype(jnp.float32), precision=lax.Precision.HIGHEST)


def reference(spectra, templates, activations, h_rate, w_rate):
    scale = 1.0 / (LAGS * K)
    weights = templates.reshape(M, LAGS * K)
    data = spectra.astype(jnp.float32)
    stack = lagged(activations.astype(jnp.bfloat16))
    resid = (scale * product(weights, stack) - data).astype(jnp.bfloat16)
    prods = product(weights.T, resid)
    padded = jnp.pad(prods, ((0, 0), (0, SPAN)))
    grad_h = padded[0:K, 0:SCANS]
    for l in range(1, LAGS):
        grad_h = grad_h + padded[l * K:(l + 1) * K, l * LAG:l * LAG + SCANS]
    grad_h = scale * grad_h
    new_h = jnp.maximum(activations - h_rate[:, None] * grad_h, 0.0)
    stack_new = lagged(new_h.astype(jnp.bfloat16))
    resid_new = (scale * product(weights, stack_new) - data).astype(jnp.bfloat16)
    grad_w = scale * product(resid_new, stack_new.T)
    rates = jnp.tile(w_rate, LAGS)[None, :]
    new_w = jnp.maximum(weights.astype(jnp.float32) - rates * grad_w, 0.0).astype(jnp.bfloat16)
    return new_h, new_w.reshape(N_MZ, M // N_MZ, LAGS * K)
```

```python
import functools
import math

import jax
import jax.numpy as jnp
from jax import lax
from jax.experimental import pallas as pl
from jax.experimental.pallas import tpu as pltpu
from jax.sharding import PartitionSpec as P

LAG = 64
PAIR = 2 * LAG

SWAP = [(0, 1), (1, 0)]


def aligned(start):
    return pl.multiple_of(start, PAIR)


def row_tile(rows):
    return rows if rows <= 256 else math.gcd(rows, 256)


def fill_stack(core, mine, other, pairs, pad):
    blocks, comps, half = mine.shape
    pairs[:, :pad] = jnp.zeros((2 * comps, pad), pairs.dtype)

    def put(first, second):
        def one(b, _):
            at = pad + b * 2 * half
            pairs[:comps, pl.ds(aligned(at), half)] = first[b]
            pairs[:comps, pl.ds(aligned(at + half), half)] = second[b]
            return 0

        lax.fori_loop(0, blocks, one, 0)

    @pl.when(core == 0)
    def _():
        put(mine, other)

    @pl.when(core == 1)
    def _():
        put(other, mine)

    width = 2 * half

    def shift(b, _):
        at = pad + b * width
        wide = pairs[:comps, pl.ds(aligned(at - PAIR), width + PAIR)]
        pairs[comps:, pl.ds(aligned(at), width)] = wide[:, PAIR - LAG : PAIR - LAG + width]
        return 0

    lax.fori_loop(0, blocks, shift, 0)


def lagged_tile(pairs, start, width, count):
    return jnp.concatenate(
        [pairs[:, pl.ds(aligned(start - p * PAIR), width)] for p in range(count)], 0
    )


def first_kernel(scale, pad, core, w, wt, mine, other, data, out, pairs, total, resid):
    j = pl.program_id(0)
    blocks = pl.num_programs(0)
    rows, lagrows = w.shape
    comps = mine.shape[1]
    width = data.shape[2]
    count = lagrows // (2 * comps)

    @pl.when(j == 0)
    def _():
        fill_stack(core[0], mine, other, pairs, pad)
        total[...] = jnp.zeros_like(total)

    at = pad + j * width
    stack = lagged_tile(pairs, at, width, count)
    tile = row_tile(rows)
    for r in range(0, rows, tile):
        recon = jnp.dot(w[r : r + tile, :], stack, preferred_element_type=jnp.float32)
        resid[r : r + tile, :] = (
            scale * recon - data[0, r : r + tile, :].astype(jnp.float32)
        ).astype(jnp.bfloat16)
    for p in range(count):
        prods = jnp.dot(
            wt[p * 2 * comps : (p + 1) * 2 * comps, :], resid[...], preferred_element_type=jnp.float32
        )
        total[:, pl.ds(aligned(at - p * PAIR), width)] += prods

    @pl.when(j == blocks - 1)
    def _():
        half = width // 2

        def one(b, _):
            for h in range(2):
                start = pad + b * width + h * half
                wide = total[comps:, pl.ds(aligned(start), half + PAIR)]
                out[h, b] = total[:comps, pl.ds(aligned(start), half)] + wide[:, LAG : LAG + half]
            return 0

        lax.fori_loop(0, out.shape[1], one, 0)


def second_kernel(scale, pad, core, w, rates, mine, other, data, out, pairs, total):
    j = pl.program_id(0)
    blocks = pl.num_programs(0)
    rows, lagrows = w.shape
    comps = mine.shape[1]
    width = data.shape[2]
    count = lagrows // (2 * comps)

    @pl.when(j == 0)
    def _():
        fill_stack(core[0], mine, other, pairs, pad)
        total[...] = jnp.zeros_like(total)

    stack = lagged_tile(pairs, pad + j * width, width, count)
    tile = row_tile(rows)
    for r in range(0, rows, tile):
        recon = jnp.dot(w[r : r + tile, :], stack, preferred_element_type=jnp.float32)
        resid = (scale * recon - data[0, r : r + tile, :].astype(jnp.float32)).astype(jnp.bfloat16)
        total[r : r + tile, :] += lax.dot_general(
            resid, stack, (((1,), (1,)), ((), ())), preferred_element_type=jnp.float32
        )

    @pl.when(j == blocks - 1)
    def _():
        for r in range(0, rows, tile):
            kept = w[r : r + tile, :].astype(jnp.float32)
            out[r : r + tile, :] = jnp.maximum(
                kept - rates[...] * (scale * total[r : r + tile, :]), 0.0
            ).astype(jnp.bfloat16)


def whole(shape):
    return pl.BlockSpec(shape, lambda j: (0,) * len(shape))


def gathered(x, count):
    copies = jnp.broadcast_to(x[None], (count,) + x.shape)
    return lax.all_to_all(copies, "scan", 0, 0, tiled=True)


def per_device(spectra, templates, activations, h_rate, w_rate):
    count = lax.axis_size("scan")
    core = lax.axis_index("mz")
    rows, lagrows = templates.shape[1:]
    comps, width = activations.shape
    half = width // 2
    scale = 1.0 / lagrows
    lags = lagrows // comps
    pad = -(-lags * LAG // PAIR) * PAIR
    core_id = core.astype(jnp.int32)[None]

    own = templates.reshape(rows, lagrows)
    own_t = own.T
    act_half = lax.dynamic_slice(activations, (0, core * half), (comps, half))
    mine = gathered(act_half.astype(jnp.bfloat16), count)
    other = lax.ppermute(mine, "mz", SWAP)
    data = lax.all_to_all(spectra.reshape(count, rows, width), "scan", 0, 0, tiled=True)

    stack_shape = pltpu.VMEM((2 * comps, pad + count * width), jnp.bfloat16)
    smem = pl.BlockSpec(memory_space=pltpu.SMEM)
    flops = 4 * rows * lagrows * width * count
    cost = pl.CostEstimate(
        flops=flops, bytes_accessed=2 * rows * width * count, transcendentals=0
    )
    partial = pl.pallas_call(
        functools.partial(first_kernel, scale, pad),
        grid=(count,),
        out_shape=jax.ShapeDtypeStruct((2, count, comps, half), jnp.float32),
        in_specs=[
            smem,
            whole((rows, lagrows)),
            whole((lagrows, rows)),
            whole((count, comps, half)),
            whole((count, comps, half)),
            pl.BlockSpec((1, rows, width), lambda j: (j, 0, 0)),
        ],
        out_specs=whole((2, count, comps, half)),
        scratch_shapes=[
            stack_shape,
            pltpu.VMEM((2 * comps, pad + count * width + PAIR), jnp.float32),
            pltpu.VMEM((rows, width), jnp.bfloat16),
        ],
        cost_estimate=cost,
        compiler_params=pltpu.CompilerParams(dimension_semantics=("arbitrary",)),
        name="first",
    )(core_id, own, own_t, mine, other, data)

    keep = lax.dynamic_index_in_dim(partial, core, 0, keepdims=False)
    give = lax.dynamic_index_in_dim(partial, 1 - core, 0, keepdims=False)
    both = keep + lax.ppermute(give, "mz", SWAP)
    pieces = lax.all_to_all(both, "scan", 0, 0, tiled=True)
    grad = scale * jnp.sum(pieces, 0)
    new_half = jnp.maximum(act_half - h_rate[:, None] * grad, 0.0)
    mine_new = gathered(new_half.astype(jnp.bfloat16), count)
    other_new = lax.ppermute(mine_new, "mz", SWAP)
    new_other = lax.ppermute(new_half, "mz", SWAP)
    new_h = jnp.where(
        core == 0,
        jnp.concatenate([new_half, new_other], 1),
        jnp.concatenate([new_other, new_half], 1),
    )

    rates = jnp.tile(w_rate, lags)[None, :]
    new_w = pl.pallas_call(
        functools.partial(second_kernel, scale, pad),
        grid=(count,),
        out_shape=jax.ShapeDtypeStruct((rows, lagrows), jnp.bfloat16),
        in_specs=[
            smem,
            whole((rows, lagrows)),
            whole((1, lagrows)),
            whole((count, comps, half)),
            whole((count, comps, half)),
            pl.BlockSpec((1, rows, width), lambda j: (j, 0, 0)),
        ],
        out_specs=whole((rows, lagrows)),
        scratch_shapes=[stack_shape, pltpu.VMEM((rows, lagrows), jnp.float32)],
        cost_estimate=cost,
        compiler_params=pltpu.CompilerParams(dimension_semantics=("arbitrary",)),
        name="second",
    )(core_id, own, rates, mine_new, other_new, data)
    return (new_h, new_w.reshape(templates.shape))


def solution(mesh):
    placed = (
        P("mz", ("slab", "scan")),
        P("mz", ("slab", "scan"), None),
        P(None, ("slab", "scan")),
        P(),
        P(),
    )
    return jax.shard_map(
        per_device,
        mesh=mesh,
        in_specs=placed,
        out_specs=(P(None, ("slab", "scan")), P("mz", ("slab", "scan"), None)),
        check_vma=False,
    )
```

```python
import functools
import math

import jax
import jax.numpy as jnp
from jax import lax
from jax.experimental import pallas as pl
from jax.experimental.pallas import tpu as pltpu
from jax.sharding import PartitionSpec as P

LAG = 64
PAIR = 2 * LAG

SWAP = [(0, 1), (1, 0)]

VMEM = pl.BlockSpec(memory_space=pltpu.VMEM)
SMEM = pl.BlockSpec(memory_space=pltpu.SMEM)
ANY = pl.BlockSpec(memory_space=pl.ANY)


def aligned(start):
    return pl.multiple_of(start, PAIR)


def row_tile(rows):
    return rows if rows <= 256 else math.gcd(rows, 256)


def fill_stack(core, place, mine, other, pairs, pad):
    blocks, comps, half = mine.shape
    width = 2 * half
    pairs[:, :pad] = jnp.zeros((2 * comps, pad), pairs.dtype)

    def put(first, second):
        def one(e, _):
            at = pad + place(e) * width
            pairs[:comps, pl.ds(aligned(at), half)] = first[e]
            pairs[:comps, pl.ds(aligned(at + half), half)] = second[e]
            return 0

        lax.fori_loop(0, blocks, one, 0)

    @pl.when(core == 0)
    def _():
        put(mine, other)

    @pl.when(core == 1)
    def _():
        put(other, mine)

    def shift(b, _):
        at = pad + b * width
        wide = pairs[:comps, pl.ds(aligned(at - PAIR), width + PAIR)]
        pairs[comps:, pl.ds(aligned(at), width)] = wide[:, PAIR - LAG : PAIR - LAG + width]
        return 0

    lax.fori_loop(0, blocks, shift, 0)


def lagged_tile(pairs, start, width, count):
    return jnp.concatenate(
        [pairs[:, pl.ds(aligned(start - p * PAIR), width)] for p in range(count)], 0
    )


def stack_kernel(pad, core, ids, mine, other, pairs):
    fill_stack(core[0], lambda e: ids[e], mine, other, pairs, pad)


def first_kernel(scale, pad, chained, core, ids, w, wt, pairs, *rest):
    before, rest = rest[: 2 * chained], rest[2 * chained :]
    datas, (give, keep, total, resid) = rest[:-4], rest[-4:]
    lagrows = w.shape[1]
    blocks, comps, half = give.shape
    rows, width = datas[0].shape
    count = lagrows // (2 * comps)
    lead = total.shape[1] - width - PAIR
    tile = row_tile(rows)
    if chained:
        give[...] = before[0][...]
        keep[...] = before[1][...]
    else:
        give[...] = jnp.zeros_like(give)
        keep[...] = jnp.zeros_like(keep)

    for i, data in enumerate(datas):
        source = ids[i]
        stack = lagged_tile(pairs, pad + source * width, width, count)
        for r in range(0, rows, tile):
            recon = jnp.dot(w[r : r + tile, :], stack, preferred_element_type=jnp.float32)
            resid[r : r + tile, :] = (
                scale * recon - data[r : r + tile, :].astype(jnp.float32)
            ).astype(jnp.bfloat16)
        total[...] = jnp.zeros_like(total)
        for p in range(count):
            prods = jnp.dot(
                wt[p * 2 * comps : (p + 1) * 2 * comps, :],
                resid[...],
                preferred_element_type=jnp.float32,
            )
            total[:, lead - p * PAIR : lead - p * PAIR + width] += prods
        back = lead // width
        for q in range(back + 1):
            block = source - back + q

            def fold(outs, q=q, block=block):
                for h in range(2):
                    start = q * width + h * half
                    outs[h][block] += (
                        total[:comps, start : start + half]
                        + total[comps:, start + LAG : start + LAG + half]
                    )

            @pl.when((block >= 0) & (core[0] == 0))
            def _():
                fold((keep, give))

            @pl.when((block >= 0) & (core[0] == 1))
            def _():
                fold((give, keep))


def second_kernel(scale, pad, core, ids, w, rate, mine, other, *rest):
    blocks, comps, half = mine.shape
    width = 2 * half
    datas, (out, pairs, total, held, sems) = rest[:blocks], rest[blocks:]
    rows, lagrows = w.shape
    count = lagrows // (2 * comps)
    tile = row_tile(rows)
    copies = [pltpu.make_async_copy(d, held.at[i], sems.at[i]) for i, d in enumerate(datas)]
    for copy in copies:
        copy.start()
    fill_stack(core[0], lambda e: e, mine, other, pairs, pad)
    total[...] = jnp.zeros_like(total)

    def one(i, _):
        pltpu.make_async_copy(held.at[i], held.at[i], sems.at[i]).wait()
        stack = lagged_tile(pairs, pad + ids[i] * width, width, count)
        for r in range(0, rows, tile):
            recon = jnp.dot(w[r : r + tile, :], stack, preferred_element_type=jnp.float32)
            resid = (scale * recon - held[i, r : r + tile, :].astype(jnp.float32)).astype(
                jnp.bfloat16
            )
            total[r : r + tile, :] += lax.dot_general(
                resid, stack, (((1,), (1,)), ((), ())), preferred_element_type=jnp.float32
            )
        return 0

    lax.fori_loop(0, blocks, one, 0)
    rates = jnp.concatenate([rate[...]] * (lagrows // comps), 1)
    for r in range(0, rows, tile):
        kept = w[r : r + tile, :].astype(jnp.float32)
        out[r : r + tile, :] = jnp.maximum(
            kept - rates * (scale * total[r : r + tile, :]), 0.0
        ).astype(jnp.bfloat16)


def cost(rows, lagrows, scans):
    return pl.CostEstimate(
        flops=4 * rows * lagrows * scans, bytes_accessed=2 * rows * scans, transcendentals=0
    )


def send_order(count):
    far = list(range(count // 2, count))
    near = list(range(2, count // 2)) + [1]
    order = []
    while far or near:
        order += far[:1] + near[:1]
        far, near = far[1:], near[1:]
    return order


def swapped(x, count, k):
    return lax.ppermute(x, "scan", [(i, i ^ k) for i in range(count)])


def gathered(x, count):
    copies = jnp.broadcast_to(x[None], (count,) + x.shape)
    return lax.all_to_all(copies, "scan", 0, 0, tiled=True)


def per_device(spectra, templates, activations, h_rate, w_rate):
    count = lax.axis_size("scan")
    me = lax.axis_index("scan").astype(jnp.int32)
    core = lax.axis_index("mz").astype(jnp.int32)
    rows, lagrows = templates.shape[1:]
    comps, width = activations.shape
    half = width // 2
    scale = 1.0 / lagrows
    lags = lagrows // comps
    pad = -(-lags * LAG // PAIR) * PAIR
    lead = -(-pad // width) * width
    core_id = core[None]

    def ids(ks):
        return me ^ jnp.array(ks, jnp.int32)

    own = templates.reshape(rows, lagrows)
    own_t = own.T
    act_half = lax.dynamic_slice(activations, (0, core * half), (comps, half))

    rounded = act_half.astype(jnp.bfloat16)
    even = list(range(0, count, 2))
    column = jnp.stack([rounded] + [swapped(rounded, count, k) for k in even[1:]])

    blocks = spectra.reshape(count, rows, width)
    order = send_order(count)
    landed = {0: lax.dynamic_index_in_dim(blocks, me, 0, keepdims=False)}
    for i, k in enumerate(order):
        block = lax.dynamic_index_in_dim(blocks, me ^ k, 0, keepdims=False)
        if i == 2:
            column, block = lax.optimization_barrier((column, block))
            beside = swapped(column, count, 1)
        landed[k] = swapped(block, count, k)

    mine = jnp.concatenate([column, beside], 0)
    other = lax.ppermute(mine, "mz", SWAP)
    stack_shape = (2 * comps, pad + count * width)
    pairs = pl.pallas_call(
        functools.partial(stack_kernel, pad),
        out_shape=jax.ShapeDtypeStruct(stack_shape, jnp.bfloat16),
        in_specs=[SMEM, SMEM, VMEM, VMEM],
        out_specs=VMEM,
        compiler_params=pltpu.CompilerParams(vmem_limit_bytes=8 << 20),
        name="stack",
    )(core_id, ids(even + [k + 1 for k in even]), mine, other)

    part = (count, comps, half)
    group = max(2, count // 4)
    groups = [[0]] + [order[i : i + group] for i in range(0, count - 1, group)]
    sums = ()
    for ks in groups:
        sums = pl.pallas_call(
            functools.partial(first_kernel, scale, pad, bool(sums)),
            out_shape=[jax.ShapeDtypeStruct(part, jnp.float32)] * 2,
            in_specs=[SMEM, SMEM] + [VMEM] * (3 + len(sums) + len(ks)),
            out_specs=[VMEM] * 2,
            scratch_shapes=[
                pltpu.VMEM((2 * comps, lead + width + PAIR), jnp.float32),
                pltpu.VMEM((rows, width), jnp.bfloat16),
            ],
            cost_estimate=cost(rows, lagrows, width * len(ks)),
            compiler_params=pltpu.CompilerParams(vmem_limit_bytes=24 << 20),
            name="first",
        )(core_id, ids(ks), own, own_t, pairs, *sums, *[landed[k] for k in ks])

    give, keep = sums
    both = keep + lax.ppermute(give, "mz", SWAP)
    pieces = lax.all_to_all(both, "scan", 0, 0, tiled=True)
    grad = scale * jnp.sum(pieces, 0)
    new_half = jnp.maximum(act_half - h_rate[:, None] * grad, 0.0)
    mine_new = gathered(new_half.astype(jnp.bfloat16), count)
    other_new = lax.ppermute(mine_new, "mz", SWAP)
    new_other = lax.ppermute(new_half, "mz", SWAP)
    new_h = jnp.where(
        core == 0,
        jnp.concatenate([new_half, new_other], 1),
        jnp.concatenate([new_other, new_half], 1),
    )

    new_w = pl.pallas_call(
        functools.partial(second_kernel, scale, pad),
        out_shape=jax.ShapeDtypeStruct((rows, lagrows), jnp.bfloat16),
        in_specs=[SMEM, SMEM] + [VMEM] * 4 + [ANY] * count,
        out_specs=VMEM,
        scratch_shapes=[
            pltpu.VMEM(stack_shape, jnp.bfloat16),
            pltpu.VMEM((rows, lagrows), jnp.float32),
            pltpu.VMEM((count, rows, width), jnp.bfloat16),
            pltpu.SemaphoreType.DMA((count,)),
        ],
        cost_estimate=cost(rows, lagrows, width * count),
        compiler_params=pltpu.CompilerParams(vmem_limit_bytes=32 << 20),
        name="second",
    )(
        core_id,
        ids([0] + order),
        own,
        w_rate[None, :],
        mine_new,
        other_new,
        *[landed[k] for k in [0] + order],
    )
    return (new_h, new_w.reshape(templates.shape))


def solution(mesh):
    placed = (
        P("mz", ("slab", "scan")),
        P("mz", ("slab", "scan"), None),
        P(None, ("slab", "scan")),
        P(),
        P(),
    )
    return jax.shard_map(
        per_device,
        mesh=mesh,
        in_specs=placed,
        out_specs=(P(None, ("slab", "scan")), P("mz", ("slab", "scan"), None)),
        check_vma=False,
    )
```

```python
import functools

import jax
import jax.numpy as jnp
from jax import lax
from jax.experimental import pallas as pl
from jax.experimental.pallas import tpu as pltpu
from jax.sharding import PartitionSpec as P


LAG = 64
PAIR = 2 * LAG

SWAP = [(0, 1), (1, 0)]

VMEM = pl.BlockSpec(memory_space=pltpu.VMEM)
SMEM = pl.BlockSpec(memory_space=pltpu.SMEM)
ANY = pl.BlockSpec(memory_space=pl.ANY)


def aligned(start):
    return pl.multiple_of(start, PAIR)


def fill_stack(core, place, mine, other, pairs, pad):
    blocks, comps, half = mine.shape
    width = 2 * half
    pairs[:, :pad] = jnp.zeros((2 * comps, pad), pairs.dtype)

    def put(first, second):
        def one(e, _):
            at = pad + place(e) * width
            pairs[:comps, pl.ds(aligned(at), half)] = first[e]
            pairs[:comps, pl.ds(aligned(at + half), half)] = second[e]
            return 0

        lax.fori_loop(0, blocks, one, 0)

    @pl.when(core == 0)
    def _():
        put(mine, other)

    @pl.when(core == 1)
    def _():
        put(other, mine)

    def shift(b, _):
        at = pad + b * width
        wide = pairs[:comps, pl.ds(aligned(at - PAIR), width + PAIR)]
        pairs[comps:, pl.ds(aligned(at), width)] = wide[:, PAIR - LAG : PAIR - LAG + width]
        return 0

    lax.fori_loop(0, blocks, shift, 0)


def lagged_tile(pairs, start, width, count):
    return jnp.concatenate(
        [pairs[:, pl.ds(aligned(start - p * PAIR), width)] for p in range(count)], 0
    )


def stack_kernel(pad, core, ids, mine, other, pairs):
    fill_stack(core[0], lambda e: ids[e], mine, other, pairs, pad)


def first_kernel(scale, pad, chained, core, ids, w, wt, pairs, *rest):
    before, rest = rest[: 2 * chained], rest[2 * chained :]
    datas, (give, keep, total, resid) = rest[:-4], rest[-4:]
    lagrows = w.shape[1]
    _, comps, half = give.shape
    _, width = datas[0].shape
    count = lagrows // (2 * comps)
    lead = total.shape[1] - width - PAIR
    if chained:
        give[...] = before[0][...]
        keep[...] = before[1][...]
    else:
        give[...] = jnp.zeros_like(give)
        keep[...] = jnp.zeros_like(keep)

    for i, data in enumerate(datas):
        source = ids[i]
        stack = lagged_tile(pairs, pad + source * width, width, count)
        recon = jnp.dot(w[...], stack, preferred_element_type=jnp.float32)
        resid[...] = (scale * recon - data[...].astype(jnp.float32)).astype(jnp.bfloat16)
        total[...] = jnp.zeros_like(total)
        prods = jnp.dot(wt[...], resid[...], preferred_element_type=jnp.float32)
        for p in range(count):
            at = lead - p * PAIR
            total[:, at : at + width] += prods[p * 2 * comps : (p + 1) * 2 * comps]
        back = lead // width
        for q in range(back + 1):
            block = source - back + q

            def fold(outs, q=q, block=block):
                for h in range(2):
                    start = q * width + h * half
                    outs[h][block] += (
                        total[:comps, start : start + half]
                        + total[comps:, start + LAG : start + LAG + half]
                    )

            @pl.when((block >= 0) & (core[0] == 0))
            def _():
                fold((keep, give))

            @pl.when((block >= 0) & (core[0] == 1))
            def _():
                fold((give, keep))


def second_kernel(scale, pad, core, ids, w, rate, mine, other, *rest):
    blocks, comps, half = mine.shape
    width = 2 * half
    datas, (out, pairs, total, held, sems) = rest[:blocks], rest[blocks:]
    _, lagrows = w.shape
    count = lagrows // (2 * comps)
    copies = [pltpu.make_async_copy(d, held.at[i], sems.at[i]) for i, d in enumerate(datas)]
    for copy in copies:
        copy.start()
    fill_stack(core[0], lambda e: e, mine, other, pairs, pad)
    total[...] = jnp.zeros_like(total)

    def one(i, _):
        pltpu.make_async_copy(held.at[i], held.at[i], sems.at[i]).wait()
        stack = lagged_tile(pairs, pad + ids[i] * width, width, count)
        recon = jnp.dot(w[...], stack, preferred_element_type=jnp.float32)
        resid = (scale * recon - held[i].astype(jnp.float32)).astype(jnp.bfloat16)
        total[...] += lax.dot_general(
            resid, stack, (((1,), (1,)), ((), ())), preferred_element_type=jnp.float32
        )
        return 0

    lax.fori_loop(0, blocks, one, 0)
    rates = jnp.concatenate([rate[...]] * (lagrows // comps), 1)
    out[...] = jnp.maximum(
        w[...].astype(jnp.float32) - rates * (scale * total[...]), 0.0
    ).astype(jnp.bfloat16)


def cost(rows, lagrows, scans):
    return pl.CostEstimate(
        flops=4 * rows * lagrows * scans, bytes_accessed=2 * rows * scans, transcendentals=0
    )


def send_order(count):
    far = list(range(count // 2, count))
    near = list(range(2, count // 2)) + [1]
    order = []
    while far or near:
        order += far[:1] + near[:1]
        far, near = far[1:], near[1:]
    return order


def sent(x, count, k):
    return lax.ppermute(x, "scan", [(i, i ^ k) for i in range(count)])


def gathered(x, count):
    copies = jnp.broadcast_to(x[None], (count,) + x.shape)
    return lax.all_to_all(copies, "scan", 0, 0, tiled=True)


def per_device(spectra, templates, activations, h_rate, w_rate):
    count = lax.axis_size("scan")
    me = lax.axis_index("scan").astype(jnp.int32)
    core = lax.axis_index("mz").astype(jnp.int32)
    rows, lagrows = templates.shape[1:]
    comps, width = activations.shape
    half = width // 2
    scale = 1.0 / lagrows
    lags = lagrows // comps
    pad = -(-lags * LAG // PAIR) * PAIR
    lead = -(-pad // width) * width
    core_id = core[None]

    def ids(ks):
        return me ^ jnp.array(ks, jnp.int32)

    own = templates.reshape(rows, lagrows)
    own_t = own.T
    act_half = lax.dynamic_slice(activations, (0, core * half), (comps, half))

    rounded = act_half.astype(jnp.bfloat16)
    even = list(range(0, count, 2))
    blocks = spectra.reshape(count, rows, width)
    order = send_order(count)
    landed = {}
    block = rounded
    for i, k in enumerate(order + [0]):
        place, block, rounded = lax.optimization_barrier((me ^ k, block, rounded))
        if i:
            landed[order[i - 1]] = sent(block, count, order[i - 1])
        if i == 1:
            column = jnp.stack([rounded] + [sent(rounded, count, e) for e in even[1:]])
        block = lax.dynamic_index_in_dim(blocks, place, 0, keepdims=False)
    landed[0] = block
    beside = sent(column, count, 1)

    mine = jnp.concatenate([column, beside], 0)
    other = lax.ppermute(mine, "mz", SWAP)
    stack_shape = (2 * comps, pad + count * width)
    pairs = pl.pallas_call(
        functools.partial(stack_kernel, pad),
        out_shape=jax.ShapeDtypeStruct(stack_shape, jnp.bfloat16),
        in_specs=[SMEM, SMEM, VMEM, VMEM],
        out_specs=VMEM,
        compiler_params=pltpu.CompilerParams(vmem_limit_bytes=8 << 20),
        name="stack",
    )(core_id, ids(even + [k + 1 for k in even]), mine, other)

    part = (count, comps, half)
    group = max(2, count // 4)
    groups = [order[i : i + group] for i in range(0, count - 2, group)] + [order[-1:]]
    groups[0] = [0] + groups[0]
    sums = ()
    for ks in groups:
        sums = pl.pallas_call(
            functools.partial(first_kernel, scale, pad, bool(sums)),
            out_shape=[jax.ShapeDtypeStruct(part, jnp.float32)] * 2,
            in_specs=[SMEM, SMEM] + [VMEM] * (3 + len(sums) + len(ks)),
            out_specs=[VMEM] * 2,
            scratch_shapes=[
                pltpu.VMEM((2 * comps, lead + width + PAIR), jnp.float32),
                pltpu.VMEM((rows, width), jnp.bfloat16),
            ],
            cost_estimate=cost(rows, lagrows, width * len(ks)),
            compiler_params=pltpu.CompilerParams(vmem_limit_bytes=24 << 20),
            name="first",
        )(core_id, ids(ks), own, own_t, pairs, *sums, *[landed[k] for k in ks])

    give, keep = sums
    both = keep + lax.ppermute(give, "mz", SWAP)
    pieces = lax.all_to_all(both, "scan", 0, 0, tiled=True)
    grad = scale * jnp.sum(pieces, 0)
    new_half = jnp.maximum(act_half - h_rate[:, None] * grad, 0.0)
    mine_new = gathered(new_half.astype(jnp.bfloat16), count)
    other_new = lax.ppermute(mine_new, "mz", SWAP)
    new_other = lax.ppermute(new_half, "mz", SWAP)
    new_h = jnp.where(
        core == 0,
        jnp.concatenate([new_half, new_other], 1),
        jnp.concatenate([new_other, new_half], 1),
    )

    new_w = pl.pallas_call(
        functools.partial(second_kernel, scale, pad),
        out_shape=jax.ShapeDtypeStruct((rows, lagrows), jnp.bfloat16),
        in_specs=[SMEM, SMEM] + [VMEM] * 4 + [ANY] * count,
        out_specs=VMEM,
        scratch_shapes=[
            pltpu.VMEM(stack_shape, jnp.bfloat16),
            pltpu.VMEM((rows, lagrows), jnp.float32),
            pltpu.VMEM((count, rows, width), jnp.bfloat16),
            pltpu.SemaphoreType.DMA((count,)),
        ],
        cost_estimate=cost(rows, lagrows, width * count),
        compiler_params=pltpu.CompilerParams(vmem_limit_bytes=32 << 20),
        name="second",
    )(
        core_id,
        ids([0] + order),
        own,
        w_rate[None, :],
        mine_new,
        other_new,
        *[landed[k] for k in [0] + order],
    )
    return (new_h, new_w.reshape(templates.shape))


def solution(mesh):
    placed = (
        P("mz", ("slab", "scan")),
        P("mz", ("slab", "scan"), None),
        P(None, ("slab", "scan")),
        P(),
        P(),
    )

    return jax.shard_map(
        per_device,
        mesh=mesh,
        in_specs=placed,
        out_specs=(P(None, ("slab", "scan")), P("mz", ("slab", "scan"), None)),
        check_vma=False,
    )
```

```python
import functools

import jax
import jax.numpy as jnp
from jax import lax
from jax.experimental import pallas as pl
from jax.experimental.pallas import tpu as pltpu
from jax.sharding import PartitionSpec as P


LAG = 64
PAIR = 2 * LAG

SWAP = [(0, 1), (1, 0)]
LIMIT = 24 << 20

VMEM = pl.BlockSpec(memory_space=pltpu.VMEM)
SMEM = pl.BlockSpec(memory_space=pltpu.SMEM)
ANY = pl.BlockSpec(memory_space=pl.ANY)


def padded_rows(rows):
    return -(-rows // PAIR) * PAIR


def late_rows(rows):
    return rows // 6 // 16 * 16


def aligned(start):
    return pl.multiple_of(start, PAIR)


def fill_stack(core, place, mine, other, pairs, pad):
    blocks, comps, half = mine.shape
    width = 2 * half
    pairs[:, :pad] = jnp.zeros((2 * comps, pad), pairs.dtype)

    def put(first, second):
        def one(e, _):
            at = pad + place(e) * width
            pairs[:comps, pl.ds(aligned(at), half)] = first[e]
            pairs[:comps, pl.ds(aligned(at + half), half)] = second[e]
            return 0

        lax.fori_loop(0, blocks, one, 0)

    @pl.when(core == 0)
    def _():
        put(mine, other)

    @pl.when(core == 1)
    def _():
        put(other, mine)

    def shift(b, _):
        at = pad + b * width
        wide = pairs[:comps, pl.ds(aligned(at - PAIR), width + PAIR)]
        pairs[comps:, pl.ds(aligned(at), width)] = wide[:, PAIR - LAG : PAIR - LAG + width]
        return 0

    lax.fori_loop(0, blocks, shift, 0)


def lagged_tile(pairs, start, width, count):
    return jnp.concatenate(
        [pairs[:, pl.ds(aligned(start - p * PAIR), width)] for p in range(count)], 0
    )


def stack_kernel(pad, core, ids, mine, other, pairs):
    fill_stack(core[0], lambda e: ids[e], mine, other, pairs, pad)


def first_kernel(scale, pad, chained, core, ids, w, wt, pairs, *rest):
    before, rest = rest[: 2 * chained], rest[2 * chained :]
    datas, (give, keep, total, resid) = rest[:-4], rest[-4:]
    lagrows = w.shape[1]
    _, comps, half = give.shape
    width = datas[0].shape[1]
    count = lagrows // (2 * comps)
    lead = total.shape[1] - width - PAIR
    if chained:
        give[...] = before[0][...]
        keep[...] = before[1][...]
    else:
        give[...] = jnp.zeros_like(give)
        keep[...] = jnp.zeros_like(keep)

    for i, data in enumerate(datas):
        source = ids[i]
        stack = lagged_tile(pairs, pad + source * width, width, count)
        rows = data.shape[0]
        padded = padded_rows(rows)
        recon = jnp.dot(w[:rows, :], stack, preferred_element_type=jnp.float32)
        resid[:rows, :] = (scale * recon - data[...].astype(jnp.float32)).astype(jnp.bfloat16)
        if padded > rows:
            resid[rows:padded, :] = jnp.zeros((padded - rows, width), jnp.bfloat16)
        total[...] = jnp.zeros_like(total)
        prods = jnp.dot(wt[:, :padded], resid[:padded, :], preferred_element_type=jnp.float32)
        for p in range(count):
            at = lead - p * PAIR
            total[:, at : at + width] += prods[p * 2 * comps : (p + 1) * 2 * comps]
        back = lead // width
        for q in range(back + 1):
            block = source - back + q

            def fold(outs, q=q, block=block):
                for h in range(2):
                    start = q * width + h * half
                    outs[h][block] += (
                        total[:comps, start : start + half]
                        + total[comps:, start + LAG : start + LAG + half]
                    )

            @pl.when((block >= 0) & (core[0] == 0))
            def _():
                fold((keep, give))

            @pl.when((block >= 0) & (core[0] == 1))
            def _():
                fold((give, keep))


def step_two(scale, w, stack, data, total):
    recon = jnp.dot(w, stack, preferred_element_type=jnp.float32)
    resid = (scale * recon - data.astype(jnp.float32)).astype(jnp.bfloat16)
    total[...] += lax.dot_general(
        resid, stack, (((1,), (1,)), ((), ())), preferred_element_type=jnp.float32
    )


def fetch(sources, held, sems):
    for i, source in enumerate(sources):
        pltpu.make_async_copy(source, held.at[i], sems.at[i]).start()


def late_kernel(scale, pad, early, core, ids, w, mine, other, *rest):
    comps, half = mine.shape[1:]
    width = 2 * half
    spectra, (pairs, kept, given, total, held, sems) = rest[:-6], rest[-6:]
    late, lagrows = kept.shape
    count = lagrows // (2 * comps)
    fetch([data.at[early : early + 2 * late, :] for data in spectra], held, sems)
    fill_stack(core[0], lambda e: e, mine, other, pairs, pad)
    total[...] = jnp.zeros_like(total)

    def one(i, _):
        pltpu.make_async_copy(held.at[i], held.at[i], sems.at[i]).wait()
        stack = lagged_tile(pairs, pad + ids[i] * width, width, count)
        step_two(scale, w[early : early + 2 * late, :], stack, held[i], total)
        return 0

    lax.fori_loop(0, len(spectra), one, 0)
    kept[...] = total[:late, :]
    given[...] = total[late:, :]


def second_kernel(scale, pad, early, ids, w, rate, pairs, *rest):
    spectra, (out, total, held, sems) = rest[:-4], rest[-4:]
    lagrows = w.shape[1]
    comps = rate.shape[1]
    width = spectra[0].shape[1]
    count = lagrows // (2 * comps)
    fetch([data.at[:early, :] for data in spectra], held, sems)
    total[...] = jnp.zeros_like(total)

    def one(i, _):
        pltpu.make_async_copy(held.at[i], held.at[i], sems.at[i]).wait()
        stack = lagged_tile(pairs, pad + ids[i] * width, width, count)
        step_two(scale, w[:early, :], stack, held[i], total)
        return 0

    lax.fori_loop(0, len(spectra), one, 0)
    rates = jnp.concatenate([rate[...]] * (lagrows // comps), 1)
    out[:early, :] = jnp.maximum(
        w[:early, :].astype(jnp.float32) - rates * (scale * total[...]), 0.0
    ).astype(jnp.bfloat16)


def cost(rows, lagrows, scans):
    return pl.CostEstimate(
        flops=4 * rows * lagrows * scans, bytes_accessed=2 * rows * scans, transcendentals=0
    )


def send_order(count):
    far = list(range(count // 2, count))
    near = list(range(2, count // 2)) + [1]
    order = []
    while far or near:
        order += far[:1] + near[:1]
        far, near = far[1:], near[1:]
    return order


def sent(x, count, k):
    return lax.ppermute(x, "scan", [(i, i ^ k) for i in range(count)])


def gathered(x, count):
    copies = jnp.broadcast_to(x[None], (count,) + x.shape)
    return lax.all_to_all(copies, "scan", 0, 0, tiled=True)


def per_device(spectra, templates, activations, h_rate, w_rate):
    count = lax.axis_size("scan")
    me = lax.axis_index("scan").astype(jnp.int32)
    core = lax.axis_index("mz").astype(jnp.int32)
    rows, lagrows = templates.shape[1:]
    comps, width = activations.shape
    half = width // 2
    scale = 1.0 / lagrows
    lags = lagrows // comps
    pad = -(-lags * LAG // PAIR) * PAIR
    lead = -(-pad // width) * width
    core_id = core[None]

    def ids(ks):
        return me ^ jnp.array(ks, jnp.int32)

    own = templates.reshape(rows, lagrows)
    act_half = lax.dynamic_slice(activations, (0, core * half), (comps, half))
    across = count // 2
    late = late_rows(rows)
    early = rows - late

    rounded = act_half.astype(jnp.bfloat16)
    even = list(range(0, count, 2))
    blocks = spectra.reshape(count, rows, width)
    order = send_order(count)
    landed = {}
    block = rounded
    for i, k in enumerate(order + [0]):
        place, block, rounded = lax.optimization_barrier((me ^ k, block, rounded))
        if i:
            landed[order[i - 1]] = sent(block, count, order[i - 1])
        if i == 1:
            column = jnp.stack([rounded] + [sent(rounded, count, e) for e in even[1:]])
            theirs = sent(own[early:], count, across)
        if k >= across:
            block = lax.dynamic_slice(blocks, (place, 0, 0), (1, early, width))[0]
        else:
            block = lax.dynamic_index_in_dim(blocks, place, 0, keepdims=False)
            extra = lax.dynamic_slice(blocks, (place ^ across, early, 0), (1, late, width))[0]
            block = jnp.concatenate([block, extra], 0)
    landed[0] = block
    beside = sent(column, count, 1)
    blank = jnp.zeros((padded_rows(rows + late) - rows - late, lagrows), jnp.bfloat16)
    all_rows = jnp.concatenate([own, theirs, blank], 0)
    all_rows_t = all_rows.T

    mine = jnp.concatenate([column, beside], 0)
    other = lax.ppermute(mine, "mz", SWAP)
    stack_shape = (2 * comps, pad + count * width)
    pairs = pl.pallas_call(
        functools.partial(stack_kernel, pad),
        out_shape=jax.ShapeDtypeStruct(stack_shape, jnp.bfloat16),
        in_specs=[SMEM, SMEM, VMEM, VMEM],
        out_specs=VMEM,
        compiler_params=pltpu.CompilerParams(vmem_limit_bytes=8 << 20),
        name="stack",
    )(core_id, ids(even + [k + 1 for k in even]), mine, other)

    part = (count, comps, half)
    group = max(2, count // 4)
    groups = [order[i : i + group] for i in range(0, count - 2, group)] + [order[-1:]]
    groups[0] = [0] + groups[0]
    sums = ()
    for ks in groups:
        call = pl.pallas_call(
            functools.partial(first_kernel, scale, pad, bool(sums)),
            out_shape=[jax.ShapeDtypeStruct(part, jnp.float32)] * 2,
            in_specs=[SMEM, SMEM] + [VMEM] * (3 + len(sums) + len(ks)),
            out_specs=[VMEM] * 2,
            scratch_shapes=[
                pltpu.VMEM((2 * comps, lead + width + PAIR), jnp.float32),
                pltpu.VMEM((all_rows.shape[0], width), jnp.bfloat16),
            ],
            cost_estimate=cost(rows, lagrows, width * len(ks)),
            compiler_params=pltpu.CompilerParams(vmem_limit_bytes=LIMIT),
            name="first",
        )
        data = [landed[k] for k in ks]
        sums = call(core_id, ids(ks), all_rows, all_rows_t, pairs, *sums, *data)

    give, keep = sums
    both = keep + lax.ppermute(give, "mz", SWAP)
    pieces = lax.all_to_all(both, "scan", 0, 0, tiled=True)
    grad = scale * jnp.sum(pieces, 0)
    new_half = jnp.maximum(act_half - h_rate[:, None] * grad, 0.0)
    mine_new = gathered(new_half.astype(jnp.bfloat16), count)
    other_new = lax.ppermute(mine_new, "mz", SWAP)
    new_other = lax.ppermute(new_half, "mz", SWAP)
    new_h = jnp.where(
        core == 0,
        jnp.concatenate([new_half, new_other], 1),
        jnp.concatenate([new_other, new_half], 1),
    )

    near = [0] + [k for k in order if k < across]
    sums_shape = jax.ShapeDtypeStruct((late, lagrows), jnp.float32)
    pairs_new, kept, given = pl.pallas_call(
        functools.partial(late_kernel, scale, pad, early),
        out_shape=[jax.ShapeDtypeStruct(stack_shape, jnp.bfloat16), sums_shape, sums_shape],
        in_specs=[SMEM, SMEM] + [VMEM] * 3 + [ANY] * len(near),
        out_specs=[VMEM] * 3,
        scratch_shapes=[
            pltpu.VMEM((2 * late, lagrows), jnp.float32),
            pltpu.VMEM((len(near), 2 * late, width), jnp.bfloat16),
            pltpu.SemaphoreType.DMA((len(near),)),
        ],
        cost_estimate=cost(2 * late, lagrows, width * len(near)),
        compiler_params=pltpu.CompilerParams(vmem_limit_bytes=LIMIT),
        name="late",
    )(core_id, ids(near), all_rows, mine_new, other_new, *[landed[k] for k in near])
    taken = sent(given, count, across)

    use = [0] + order
    second = pl.pallas_call(
        functools.partial(second_kernel, scale, pad, early),
        out_shape=jax.ShapeDtypeStruct((rows, lagrows), jnp.bfloat16),
        in_specs=[SMEM] + [VMEM] * 3 + [ANY] * count,
        out_specs=VMEM,
        scratch_shapes=[
            pltpu.VMEM((early, lagrows), jnp.float32),
            pltpu.VMEM((count, early, width), jnp.bfloat16),
            pltpu.SemaphoreType.DMA((count,)),
        ],
        cost_estimate=cost(early, lagrows, width * count),
        compiler_params=pltpu.CompilerParams(vmem_limit_bytes=LIMIT),
        name="second",
    )
    new_w = second(ids(use), all_rows, w_rate[None, :], pairs_new, *[landed[k] for k in use])
    rates = jnp.tile(w_rate, lags)[None, :]
    new_late = own[early:].astype(jnp.float32) - rates * (scale * (kept + taken))
    new_w = lax.dynamic_update_slice(
        new_w, jnp.maximum(new_late, 0.0).astype(jnp.bfloat16), (early, 0)
    )
    return (new_h, new_w.reshape(templates.shape))


def solution(mesh):
    placed = (
        P("mz", ("slab", "scan")),
        P("mz", ("slab", "scan"), None),
        P(None, ("slab", "scan")),
        P(),
        P(),
    )

    return jax.shard_map(
        per_device,
        mesh=mesh,
        in_specs=placed,
        out_specs=(P(None, ("slab", "scan")), P("mz", ("slab", "scan"), None)),
        check_vma=False,
    )
```

```python
import functools

import jax
import jax.numpy as jnp
from jax import lax
from jax.experimental import pallas as pl
from jax.experimental.pallas import tpu as pltpu
from jax.sharding import PartitionSpec as P


LAG = 64
PAIR = 2 * LAG

SWAP = [(0, 1), (1, 0)]
LIMIT = 20 << 20

VMEM = pl.BlockSpec(memory_space=pltpu.VMEM)
SMEM = pl.BlockSpec(memory_space=pltpu.SMEM)
ANY = pl.BlockSpec(memory_space=pl.ANY)


def padded_rows(rows):
    return -(-rows // PAIR) * PAIR


def late_rows(rows):
    return rows // 6 // 16 * 16


def aligned(start):
    return pl.multiple_of(start, PAIR)


def fill_stack(core, place, mine, other, pairs, pad):
    blocks, comps, half = mine.shape
    width = 2 * half
    pairs[:, :pad] = jnp.zeros((2 * comps, pad), pairs.dtype)

    def put(first, second):
        def one(e, _):
            at = pad + place(e) * width
            pairs[:comps, pl.ds(aligned(at), half)] = first[e]
            pairs[:comps, pl.ds(aligned(at + half), half)] = second[e]
            return 0

        lax.fori_loop(0, blocks, one, 0, unroll=blocks <= 8)

    @pl.when(core == 0)
    def _():
        put(mine, other)

    @pl.when(core == 1)
    def _():
        put(other, mine)

    def shift(b, _):
        at = pad + b * width
        wide = pairs[:comps, pl.ds(aligned(at - PAIR), width + PAIR)]
        pairs[comps:, pl.ds(aligned(at), width)] = wide[:, PAIR - LAG : PAIR - LAG + width]
        return 0

    lax.fori_loop(0, blocks, shift, 0, unroll=blocks <= 8)


def lagged_tile(pairs, start, width, count):
    return jnp.concatenate(
        [pairs[:, pl.ds(aligned(start - p * PAIR), width)] for p in range(count)], 0
    )


def stack_kernel(pad, core, ids, mine, other, pairs):
    fill_stack(core[0], lambda e: ids[e], mine, other, pairs, pad)


def first_kernel(scale, pad, chained, core, ids, w, wt, pairs, *rest):
    before, rest = rest[: 2 * chained], rest[2 * chained :]
    datas, (give, keep, total, resid) = rest[:-4], rest[-4:]
    lagrows = w.shape[1]
    _, comps, half = give.shape
    width = datas[0].shape[1]
    count = lagrows // (2 * comps)
    lead = total.shape[1] - width - PAIR
    if chained:
        give[...] = before[0][...]
        keep[...] = before[1][...]
    else:
        give[...] = jnp.zeros_like(give)
        keep[...] = jnp.zeros_like(keep)

    for i, data in enumerate(datas):
        source = ids[i]
        stack = lagged_tile(pairs, pad + source * width, width, count)
        rows = data.shape[0]
        padded = padded_rows(rows)
        recon = jnp.dot(w[:rows, :], stack, preferred_element_type=jnp.float32)
        resid[:rows, :] = (scale * recon - data[...].astype(jnp.float32)).astype(jnp.bfloat16)
        if padded > rows:
            resid[rows:padded, :] = jnp.zeros((padded - rows, width), jnp.bfloat16)
        total[...] = jnp.zeros_like(total)
        prods = jnp.dot(wt[:, :padded], resid[:padded, :], preferred_element_type=jnp.float32)
        for p in range(count):
            at = lead - p * PAIR
            total[:, at : at + width] += prods[p * 2 * comps : (p + 1) * 2 * comps]
        back = lead // width
        for q in range(back + 1):
            block = source - back + q

            def fold(outs, q=q, block=block):
                for h in range(2):
                    start = q * width + h * half
                    outs[h][block] += (
                        total[:comps, start : start + half]
                        + total[comps:, start + LAG : start + LAG + half]
                    )

            @pl.when((block >= 0) & (core[0] == 0))
            def _():
                fold((keep, give))

            @pl.when((block >= 0) & (core[0] == 1))
            def _():
                fold((give, keep))


def step_two(scale, w, stack, data, total):
    recon = jnp.dot(w, stack, preferred_element_type=jnp.float32)
    resid = (scale * recon - data.astype(jnp.float32)).astype(jnp.bfloat16)
    total[...] += lax.dot_general(
        resid, stack, (((1,), (1,)), ((), ())), preferred_element_type=jnp.float32
    )


def fetch(sources, held, sems):
    for i, source in enumerate(sources):
        pltpu.make_async_copy(source, held.at[i], sems.at[i]).start()


def late_kernel(scale, pad, early, core, ids, w, mine, other, *rest):
    comps, half = mine.shape[1:]
    width = 2 * half
    spectra, (pairs, kept, given, total, held, sems) = rest[:-6], rest[-6:]
    late, lagrows = kept.shape
    count = lagrows // (2 * comps)
    fetch([data.at[early : early + 2 * late, :] for data in spectra], held, sems)
    fill_stack(core[0], lambda e: e, mine, other, pairs, pad)
    total[...] = jnp.zeros_like(total)

    def one(i, _):
        pltpu.make_async_copy(held.at[i], held.at[i], sems.at[i]).wait()
        stack = lagged_tile(pairs, pad + ids[i] * width, width, count)
        step_two(scale, w[early : early + 2 * late, :], stack, held[i], total)
        return 0

    lax.fori_loop(0, len(spectra), one, 0)
    kept[...] = total[:late, :]
    given[...] = total[late:, :]


def second_kernel(scale, pad, early, ids, w, rate, pairs, *rest):
    spectra, (out, total, held, sems) = rest[:-4], rest[-4:]
    lagrows = w.shape[1]
    comps = rate.shape[1]
    width = spectra[0].shape[1]
    count = lagrows // (2 * comps)
    fetch([data.at[:early, :] for data in spectra], held, sems)
    total[...] = jnp.zeros_like(total)

    def one(i, _):
        pltpu.make_async_copy(held.at[i], held.at[i], sems.at[i]).wait()
        stack = lagged_tile(pairs, pad + ids[i] * width, width, count)
        step_two(scale, w[:early, :], stack, held[i], total)
        return 0

    lax.fori_loop(0, len(spectra), one, 0)
    rates = jnp.concatenate([rate[...]] * (lagrows // comps), 1)
    out[:early, :] = jnp.maximum(
        w[:early, :].astype(jnp.float32) - rates * (scale * total[...]), 0.0
    ).astype(jnp.bfloat16)


def final_kernel(scale, early, before, w, rate, kept, taken, out, held, sem):
    del before
    rates = jnp.concatenate([rate[...]] * (w.shape[1] // rate.shape[1]), 1)
    grad = scale * (kept[...] + taken[...])
    held[...] = jnp.maximum(w[early:, :].astype(jnp.float32) - rates * grad, 0.0).astype(
        jnp.bfloat16
    )
    copy = pltpu.make_async_copy(held, out.at[early:, :], sem)
    copy.start()
    copy.wait()


def update_kernel(scale, pieces, old, rate, new, copies):
    grad = scale * jnp.sum(pieces[...], 0)
    value = jnp.maximum(old[...] - rate[...] * grad, 0.0)
    new[...] = value
    rounded = value.astype(jnp.bfloat16)
    for i in range(copies.shape[0]):
        copies[i] = rounded


def cost(rows, lagrows, scans):
    return pl.CostEstimate(
        flops=4 * rows * lagrows * scans, bytes_accessed=2 * rows * scans, transcendentals=0
    )


def send_order(count):
    far = list(range(count // 2, count))
    near = list(range(2, count // 2)) + [1]
    order = []
    while far or near:
        order += far[:1] + near[:1]
        far, near = far[1:], near[1:]
    return order


def sent(x, count, k):
    return lax.ppermute(x, "scan", [(i, i ^ k) for i in range(count)])


def per_device(spectra, templates, activations, h_rate, w_rate):
    count = lax.axis_size("scan")
    me = lax.axis_index("scan").astype(jnp.int32)
    core = lax.axis_index("mz").astype(jnp.int32)
    rows, lagrows = templates.shape[1:]
    comps, width = activations.shape
    half = width // 2
    scale = 1.0 / lagrows
    lags = lagrows // comps
    pad = -(-lags * LAG // PAIR) * PAIR
    lead = -(-pad // width) * width
    core_id = core[None]

    def ids(ks):
        return me ^ jnp.array(ks, jnp.int32)

    own = templates.reshape(rows, lagrows)
    across = count // 2
    late = late_rows(rows)
    early = rows - late

    act_half = lax.dynamic_slice(activations, (0, core * half), (comps, half))
    rounded = act_half.astype(jnp.bfloat16)
    even = list(range(0, count, 2))
    blocks = spectra.reshape(count, rows, width)
    order = send_order(count)
    landed = {}
    for i, k in enumerate(order + [0]):
        place = me ^ k
        if i:
            place, block = lax.optimization_barrier((place, block))
            landed[order[i - 1]] = sent(block, count, order[i - 1])
        if i == 1:
            column = jnp.stack([rounded] + [sent(rounded, count, e) for e in even[1:]])
            theirs = sent(own[early:], count, across)
        if k >= across:
            block = lax.dynamic_slice(blocks, (place, 0, 0), (1, early, width))[0]
        else:
            block = lax.dynamic_index_in_dim(blocks, place, 0, keepdims=False)
            extra = lax.dynamic_slice(blocks, (place ^ across, early, 0), (1, late, width))[0]
            block = jnp.concatenate([block, extra], 0)
    landed[0] = block
    beside = sent(column, count, 1)
    blank = jnp.zeros((padded_rows(rows + late) - rows - late, lagrows), jnp.bfloat16)
    all_rows = jnp.concatenate([own, theirs, blank], 0)
    all_rows_t = all_rows.T

    mine = jnp.concatenate([column, beside], 0)
    other = lax.ppermute(mine, "mz", SWAP)
    stack_shape = (2 * comps, pad + count * width)
    pairs = pl.pallas_call(
        functools.partial(stack_kernel, pad),
        out_shape=jax.ShapeDtypeStruct(stack_shape, jnp.bfloat16),
        in_specs=[SMEM, SMEM, VMEM, VMEM],
        out_specs=VMEM,
        compiler_params=pltpu.CompilerParams(vmem_limit_bytes=8 << 20),
        name="stack",
    )(core_id, ids(even + [k + 1 for k in even]), mine, other)

    part = (count, comps, half)
    group = max(2, count // 4)
    groups = [order[i : i + group] for i in range(0, count - 2, group)] + [order[-1:]]
    groups[0] = [0] + groups[0]
    sums = ()
    for ks in groups:
        call = pl.pallas_call(
            functools.partial(first_kernel, scale, pad, bool(sums)),
            out_shape=[jax.ShapeDtypeStruct(part, jnp.float32)] * 2,
            in_specs=[SMEM, SMEM] + [VMEM] * (3 + len(sums) + len(ks)),
            out_specs=[VMEM] * 2,
            scratch_shapes=[
                pltpu.VMEM((2 * comps, lead + width + PAIR), jnp.float32),
                pltpu.VMEM((all_rows.shape[0], width), jnp.bfloat16),
            ],
            cost_estimate=cost(rows, lagrows, width * len(ks)),
            compiler_params=pltpu.CompilerParams(vmem_limit_bytes=LIMIT),
            name="first",
        )
        data = [landed[k] for k in ks]
        sums = call(core_id, ids(ks), all_rows, all_rows_t, pairs, *sums, *data)

    give, keep = sums
    both = keep + lax.ppermute(give, "mz", SWAP)
    pieces = lax.all_to_all(both, "scan", 0, 0, tiled=True)
    new_half, copies = pl.pallas_call(
        functools.partial(update_kernel, scale),
        out_shape=[
            jax.ShapeDtypeStruct((comps, half), jnp.float32),
            jax.ShapeDtypeStruct(part, jnp.bfloat16),
        ],
        in_specs=[VMEM] * 3,
        out_specs=[VMEM] * 2,
        compiler_params=pltpu.CompilerParams(vmem_limit_bytes=8 << 20),
        name="update",
    )(pieces, act_half, h_rate[:, None])
    mine_new = lax.all_to_all(copies, "scan", 0, 0, tiled=True)
    other_new = lax.ppermute(mine_new, "mz", SWAP)
    new_other = lax.ppermute(new_half, "mz", SWAP)
    new_h = jnp.where(
        core == 0,
        jnp.concatenate([new_half, new_other], 1),
        jnp.concatenate([new_other, new_half], 1),
    )

    near = [0] + [k for k in order if k < across]
    sums_shape = jax.ShapeDtypeStruct((late, lagrows), jnp.float32)
    pairs_new, kept, given = pl.pallas_call(
        functools.partial(late_kernel, scale, pad, early),
        out_shape=[jax.ShapeDtypeStruct(stack_shape, jnp.bfloat16), sums_shape, sums_shape],
        in_specs=[SMEM, SMEM] + [VMEM] * 3 + [ANY] * len(near),
        out_specs=[VMEM] * 3,
        scratch_shapes=[
            pltpu.VMEM((2 * late, lagrows), jnp.float32),
            pltpu.VMEM((len(near), 2 * late, width), jnp.bfloat16),
            pltpu.SemaphoreType.DMA((len(near),)),
        ],
        cost_estimate=cost(2 * late, lagrows, width * len(near)),
        compiler_params=pltpu.CompilerParams(vmem_limit_bytes=LIMIT),
        name="late",
    )(core_id, ids(near), all_rows, mine_new, other_new, *[landed[k] for k in near])
    taken = sent(given, count, across)

    use = [0] + order
    second = pl.pallas_call(
        functools.partial(second_kernel, scale, pad, early),
        out_shape=jax.ShapeDtypeStruct((rows, lagrows), jnp.bfloat16),
        in_specs=[SMEM] + [VMEM] * 3 + [ANY] * count,
        out_specs=VMEM,
        scratch_shapes=[
            pltpu.VMEM((early, lagrows), jnp.float32),
            pltpu.VMEM((count, early, width), jnp.bfloat16),
            pltpu.SemaphoreType.DMA((count,)),
        ],
        cost_estimate=cost(early, lagrows, width * count),
        compiler_params=pltpu.CompilerParams(vmem_limit_bytes=LIMIT),
        name="second",
    )
    new_w = second(ids(use), all_rows, w_rate[None, :], pairs_new, *[landed[k] for k in use])
    new_w = pl.pallas_call(
        functools.partial(final_kernel, scale, early),
        out_shape=jax.ShapeDtypeStruct((rows, lagrows), jnp.bfloat16),
        in_specs=[ANY] + [VMEM] * 4,
        out_specs=ANY,
        scratch_shapes=[pltpu.VMEM((late, lagrows), jnp.bfloat16), pltpu.SemaphoreType.DMA],
        input_output_aliases={0: 0},
        compiler_params=pltpu.CompilerParams(vmem_limit_bytes=8 << 20),
        name="final",
    )(new_w, own, w_rate[None, :], kept, taken)
    return (new_h, new_w.reshape(templates.shape))


def solution(mesh):
    placed = (
        P("mz", ("slab", "scan")),
        P("mz", ("slab", "scan"), None),
        P(None, ("slab", "scan")),
        P(),
        P(),
    )

    return jax.shard_map(
        per_device,
        mesh=mesh,
        in_specs=placed,
        out_specs=(P(None, ("slab", "scan")), P("mz", ("slab", "scan"), None)),
        check_vma=False,
    )
```

```python
import functools

import jax
import jax.numpy as jnp
from jax import lax
from jax.experimental import pallas as pl
from jax.experimental.pallas import tpu as pltpu
from jax.sharding import PartitionSpec as P


LAG = 64
PAIR = 2 * LAG

SWAP = [(0, 1), (1, 0)]
LIMIT = 20 << 20

VMEM = pl.BlockSpec(memory_space=pltpu.VMEM)
SMEM = pl.BlockSpec(memory_space=pltpu.SMEM)
ANY = pl.BlockSpec(memory_space=pl.ANY)


def padded_rows(rows):
    return -(-rows // PAIR) * PAIR


def row_parts(rows):
    mid, late = rows // 12 // 16 * 16, rows * 3 // 256 * 16
    return rows - mid - late, mid, late


def aligned(start):
    return pl.multiple_of(start, PAIR)


def fill_stack(core, place, mine, other, pairs, pad):
    blocks, comps, half = mine.shape
    width = 2 * half
    pairs[:, :pad] = jnp.zeros((2 * comps, pad), pairs.dtype)

    def put(first, second):
        def one(e, _):
            at = pad + place(e) * width
            pairs[:comps, pl.ds(aligned(at), half)] = first[e]
            pairs[:comps, pl.ds(aligned(at + half), half)] = second[e]
            return 0

        lax.fori_loop(0, blocks, one, 0, unroll=blocks <= 8)

    @pl.when(core == 0)
    def _():
        put(mine, other)

    @pl.when(core == 1)
    def _():
        put(other, mine)

    def shift(b, _):
        at = pad + b * width
        wide = pairs[:comps, pl.ds(aligned(at - PAIR), width + PAIR)]
        pairs[comps:, pl.ds(aligned(at), width)] = wide[:, PAIR - LAG : PAIR - LAG + width]
        return 0

    lax.fori_loop(0, blocks, shift, 0, unroll=blocks <= 8)


def lagged_tile(pairs, start, width, count):
    return jnp.concatenate(
        [pairs[:, pl.ds(aligned(start - p * PAIR), width)] for p in range(count)], 0
    )


def stack_kernel(pad, core, ids, mine, other, pairs):
    fill_stack(core[0], lambda e: ids[e], mine, other, pairs, pad)


def first_kernel(scale, pad, chained, core, ids, w, wt, pairs, *rest):
    before, rest = rest[: 2 * chained], rest[2 * chained :]
    datas, (give, keep, total, resid) = rest[:-4], rest[-4:]
    lagrows = w.shape[1]
    _, comps, half = give.shape
    width = datas[0].shape[1]
    count = lagrows // (2 * comps)
    lead = total.shape[1] - width - PAIR
    if chained:
        give[...] = before[0][...]
        keep[...] = before[1][...]
    else:
        give[...] = jnp.zeros_like(give)
        keep[...] = jnp.zeros_like(keep)

    for i, data in enumerate(datas):
        source = ids[i]
        stack = lagged_tile(pairs, pad + source * width, width, count)
        rows = data.shape[0]
        padded = padded_rows(rows)
        recon = jnp.dot(w[:rows, :], stack, preferred_element_type=jnp.float32)
        resid[:rows, :] = (scale * recon - data[...].astype(jnp.float32)).astype(jnp.bfloat16)
        if padded > rows:
            resid[rows:padded, :] = jnp.zeros((padded - rows, width), jnp.bfloat16)
        total[...] = jnp.zeros_like(total)
        prods = jnp.dot(wt[:, :padded], resid[:padded, :], preferred_element_type=jnp.float32)
        for p in range(count):
            at = lead - p * PAIR
            total[:, at : at + width] += prods[p * 2 * comps : (p + 1) * 2 * comps]
        back = lead // width
        for q in range(back + 1):
            block = source - back + q

            def fold(outs, q=q, block=block):
                for h in range(2):
                    start = q * width + h * half
                    outs[h][block] += (
                        total[:comps, start : start + half]
                        + total[comps:, start + LAG : start + LAG + half]
                    )

            @pl.when((block >= 0) & (core[0] == 0))
            def _():
                fold((keep, give))

            @pl.when((block >= 0) & (core[0] == 1))
            def _():
                fold((give, keep))


def step_two(scale, w, stack, data, total):
    recon = jnp.dot(w, stack, preferred_element_type=jnp.float32)
    resid = (scale * recon - data.astype(jnp.float32)).astype(jnp.bfloat16)
    total[...] += lax.dot_general(
        resid, stack, (((1,), (1,)), ((), ())), preferred_element_type=jnp.float32
    )


def fetch(sources, held, sems):
    for i, source in enumerate(sources):
        pltpu.make_async_copy(source, held.at[i], sems.at[i]).start()


def late_kernel(scale, pad, early, core, ids, w, mine, other, *rest):
    comps, half = mine.shape[1:]
    width = 2 * half
    spectra, (pairs, kept, given, total, held, sems) = rest[:-6], rest[-6:]
    late, lagrows = kept.shape
    count = lagrows // (2 * comps)
    fetch([data.at[early : early + 2 * late, :] for data in spectra], held, sems)
    fill_stack(core[0], lambda e: e, mine, other, pairs, pad)
    total[...] = jnp.zeros_like(total)

    def one(i, _):
        pltpu.make_async_copy(held.at[i], held.at[i], sems.at[i]).wait()
        stack = lagged_tile(pairs, pad + ids[i] * width, width, count)
        step_two(scale, w[early : early + 2 * late, :], stack, held[i], total)
        return 0

    lax.fori_loop(0, len(spectra), one, 0)
    kept[...] = total[:late, :]
    given[...] = total[late:, :]


def second_kernel(scale, pad, ids, w, rate, pairs, *rest):
    blocks = ids.shape[0]
    near = blocks // 2
    spectra, rest = rest[:blocks], rest[blocks:]
    crossed, (out, total, held, sems, mid_sems) = rest[:-5], rest[-5:]
    inner, lagrows = total.shape
    comps = rate.shape[1]
    early, width = spectra[near].shape
    count = lagrows // (2 * comps)
    for i, data in enumerate(spectra[:near]):
        pltpu.make_async_copy(data.at[:inner, :], held.at[i], sems.at[i]).start()
    mids = [part.at[e] for part in crossed for e in range(part.shape[0])]
    for i, (data, rows) in enumerate(zip(spectra[near:], mids)):
        pltpu.make_async_copy(data, held.at[near + i, :early, :], sems.at[near + i]).start()
        pltpu.make_async_copy(rows, held.at[near + i, early:, :], mid_sems.at[i]).start()
    total[...] = jnp.zeros_like(total)

    def one(i, _):
        @pl.when(i < near)
        def _():
            pltpu.make_async_copy(held.at[i], held.at[i], sems.at[i]).wait()

        @pl.when(i >= near)
        def _():
            head, tail = held.at[i, :early, :], held.at[i, early:, :]
            pltpu.make_async_copy(head, head, sems.at[i]).wait()
            pltpu.make_async_copy(tail, tail, mid_sems.at[i - near]).wait()

        stack = lagged_tile(pairs, pad + ids[i] * width, width, count)
        step_two(scale, w[:inner, :], stack, held[i], total)
        return 0

    lax.fori_loop(0, blocks, one, 0)
    rates = jnp.concatenate([rate[...]] * (lagrows // comps), 1)
    out[:inner, :] = jnp.maximum(
        w[:inner, :].astype(jnp.float32) - rates * (scale * total[...]), 0.0
    ).astype(jnp.bfloat16)


def final_kernel(scale, early, before, w, rate, kept, taken, out, held, sem):
    del before
    rates = jnp.concatenate([rate[...]] * (w.shape[1] // rate.shape[1]), 1)
    grad = scale * (kept[...] + taken[...])
    held[...] = jnp.maximum(w[early:, :].astype(jnp.float32) - rates * grad, 0.0).astype(
        jnp.bfloat16
    )
    copy = pltpu.make_async_copy(held, out.at[early:, :], sem)
    copy.start()
    copy.wait()


def update_kernel(scale, pieces, old, rate, new, copies):
    grad = scale * jnp.sum(pieces[...], 0)
    value = jnp.maximum(old[...] - rate[...] * grad, 0.0)
    new[...] = value
    rounded = value.astype(jnp.bfloat16)
    for i in range(copies.shape[0]):
        copies[i] = rounded


def cost(rows, lagrows, scans):
    return pl.CostEstimate(
        flops=4 * rows * lagrows * scans, bytes_accessed=2 * rows * scans, transcendentals=0
    )


def send_order(count):
    far = list(range(count // 2, count))
    near = list(range(2, count // 2)) + [1]
    order, far, near = [far[0]] + near[:2], far[1:], near[2:]
    while far or near:
        order += far[:1] + near[:1]
        far, near = far[1:], near[1:]
    return order


def sent(x, count, k):
    return lax.ppermute(x, "scan", [(i, i ^ k) for i in range(count)])


def per_device(spectra, templates, activations, h_rate, w_rate):
    count = lax.axis_size("scan")
    me = lax.axis_index("scan").astype(jnp.int32)
    core = lax.axis_index("mz").astype(jnp.int32)
    rows, lagrows = templates.shape[1:]
    comps, width = activations.shape
    half = width // 2
    scale = 1.0 / lagrows
    lags = lagrows // comps
    pad = -(-lags * LAG // PAIR) * PAIR
    lead = -(-pad // width) * width
    core_id = core[None]

    def ids(ks):
        return me ^ jnp.array(ks, jnp.int32)

    own = templates.reshape(rows, lagrows)
    across = count // 2
    early, mid, late = row_parts(rows)
    inner = early + mid

    act_half = lax.dynamic_slice(activations, (0, core * half), (comps, half))
    rounded = act_half.astype(jnp.bfloat16)
    even = list(range(0, count, 2))
    blocks = spectra.reshape(count, rows, width)
    order = send_order(count)
    landed = {}
    for i, k in enumerate(order + [0]):
        place = me ^ k
        if i:
            place, block = lax.optimization_barrier((place, block))
            landed[order[i - 1]] = sent(block, count, order[i - 1])
        if i == 1:
            column = jnp.stack([rounded] + [sent(rounded, count, e) for e in even[1:]])
            swap = jnp.concatenate([own[inner:], own[early:inner]], 0)
            theirs = sent(swap, count, across)
        if k >= across:
            block = lax.dynamic_slice(blocks, (place, 0, 0), (1, early, width))[0]
        else:
            block = lax.dynamic_index_in_dim(blocks, place, 0, keepdims=False)
            far = place ^ across
            lates = lax.dynamic_slice(blocks, (far, inner, 0), (1, late, width))[0]
            mids = lax.dynamic_slice(blocks, (far, early, 0), (1, mid, width))[0]
            block = jnp.concatenate([block, lates, mids], 0)
    landed[0] = block
    beside = sent(column, count, 1)
    stay = rows + late + mid
    blank = jnp.zeros((padded_rows(stay) - stay, lagrows), jnp.bfloat16)
    all_rows = jnp.concatenate([own, theirs, blank], 0)
    all_rows_t = all_rows.T

    mine = jnp.concatenate([column, beside], 0)
    other = lax.ppermute(mine, "mz", SWAP)
    stack_shape = (2 * comps, pad + count * width)
    pairs = pl.pallas_call(
        functools.partial(stack_kernel, pad),
        out_shape=jax.ShapeDtypeStruct(stack_shape, jnp.bfloat16),
        in_specs=[SMEM, SMEM, VMEM, VMEM],
        out_specs=VMEM,
        compiler_params=pltpu.CompilerParams(vmem_limit_bytes=8 << 20),
        name="stack",
    )(core_id, ids(even + [k + 1 for k in even]), mine, other)

    near = [0] + [k for k in order if k < across]
    near_parts = (near[: across // 2], near[across // 2 :])
    part = (count, comps, half)
    group = max(2, count // 4)
    arrival = [0] + [k for k in order if k not in (3, count - 1)] + [3, count - 1]
    singles = min(2, count)
    groups = [arrival[i : i + group] for i in range(0, count - singles, group)]
    groups += [[k] for k in arrival[-singles:]]
    sums = ()
    for i, ks in enumerate(groups):
        call = pl.pallas_call(
            functools.partial(first_kernel, scale, pad, bool(sums)),
            out_shape=[jax.ShapeDtypeStruct(part, jnp.float32)] * 2,
            in_specs=[SMEM, SMEM] + [VMEM] * (3 + len(sums) + len(ks)),
            out_specs=[VMEM] * 2,
            scratch_shapes=[
                pltpu.VMEM((2 * comps, lead + width + PAIR), jnp.float32),
                pltpu.VMEM((all_rows.shape[0], width), jnp.bfloat16),
            ],
            cost_estimate=cost(rows, lagrows, width * len(ks)),
            compiler_params=pltpu.CompilerParams(vmem_limit_bytes=LIMIT),
            name="first",
        )
        if i == len(groups) - 2:
            mids = [jnp.stack([landed[k][rows + late :] for k in near_parts[0]])]
            mids, sums = lax.optimization_barrier((mids, sums))
        data = [landed[k] for k in ks]
        sums = call(core_id, ids(ks), all_rows, all_rows_t, pairs, *sums, *data)

    give, keep = sums
    gift = lax.ppermute(give, "mz", SWAP)
    crossed = [sent(mids[0], count, across)]
    both = keep + gift
    held, both = lax.optimization_barrier(([landed[k] for k in near_parts[1]], both))
    mids.append(jnp.stack([block[rows + late :] for block in held]))
    pieces = lax.all_to_all(both, "scan", 0, 0, tiled=True)
    crossed.append(sent(mids[1], count, across))
    new_half, copies = pl.pallas_call(
        functools.partial(update_kernel, scale),
        out_shape=[
            jax.ShapeDtypeStruct((comps, half), jnp.float32),
            jax.ShapeDtypeStruct(part, jnp.bfloat16),
        ],
        in_specs=[VMEM] * 3,
        out_specs=[VMEM] * 2,
        compiler_params=pltpu.CompilerParams(vmem_limit_bytes=8 << 20),
        name="update",
    )(pieces, act_half, h_rate[:, None])
    mine_new = lax.all_to_all(copies, "scan", 0, 0, tiled=True)
    other_new = lax.ppermute(mine_new, "mz", SWAP)
    new_other = lax.ppermute(new_half, "mz", SWAP)
    new_h = jnp.where(
        core == 0,
        jnp.concatenate([new_half, new_other], 1),
        jnp.concatenate([new_other, new_half], 1),
    )

    sums_shape = jax.ShapeDtypeStruct((late, lagrows), jnp.float32)
    call = pl.pallas_call(
        functools.partial(late_kernel, scale, pad, inner),
        out_shape=[jax.ShapeDtypeStruct(stack_shape, jnp.bfloat16), sums_shape, sums_shape],
        in_specs=[SMEM, SMEM] + [VMEM] * 3 + [ANY] * len(near),
        out_specs=[VMEM] * 3,
        scratch_shapes=[
            pltpu.VMEM((2 * late, lagrows), jnp.float32),
            pltpu.VMEM((len(near), 2 * late, width), jnp.bfloat16),
            pltpu.SemaphoreType.DMA((len(near),)),
        ],
        cost_estimate=cost(2 * late, lagrows, width * len(near)),
        compiler_params=pltpu.CompilerParams(vmem_limit_bytes=LIMIT),
        name="late",
    )
    pairs_new, kept, given = call(
        core_id, ids(near), all_rows, mine_new, other_new, *[landed[k] for k in near]
    )
    taken = sent(given, count, across)

    use = near + [k + across for k in near]
    second = pl.pallas_call(
        functools.partial(second_kernel, scale, pad),
        out_shape=jax.ShapeDtypeStruct((rows, lagrows), jnp.bfloat16),
        in_specs=[SMEM] + [VMEM] * 3 + [ANY] * (count + len(crossed)),
        out_specs=VMEM,
        scratch_shapes=[
            pltpu.VMEM((inner, lagrows), jnp.float32),
            pltpu.VMEM((count, inner, width), jnp.bfloat16),
            pltpu.SemaphoreType.DMA((count,)),
            pltpu.SemaphoreType.DMA((across,)),
        ],
        cost_estimate=cost(inner, lagrows, width * count),
        compiler_params=pltpu.CompilerParams(vmem_limit_bytes=LIMIT),
        name="second",
    )
    data = [landed[k] for k in use] + crossed
    new_w = second(ids(use), all_rows, w_rate[None, :], pairs_new, *data)
    new_w = pl.pallas_call(
        functools.partial(final_kernel, scale, inner),
        out_shape=jax.ShapeDtypeStruct((rows, lagrows), jnp.bfloat16),
        in_specs=[ANY] + [VMEM] * 4,
        out_specs=ANY,
        scratch_shapes=[pltpu.VMEM((late, lagrows), jnp.bfloat16), pltpu.SemaphoreType.DMA],
        input_output_aliases={0: 0},
        compiler_params=pltpu.CompilerParams(vmem_limit_bytes=8 << 20),
        name="final",
    )(new_w, own, w_rate[None, :], kept, taken)
    return (new_h, new_w.reshape(templates.shape))


def solution(mesh):
    placed = (
        P("mz", ("slab", "scan")),
        P("mz", ("slab", "scan"), None),
        P(None, ("slab", "scan")),
        P(),
        P(),
    )

    return jax.shard_map(
        per_device,
        mesh=mesh,
        in_specs=placed,
        out_specs=(P(None, ("slab", "scan")), P("mz", ("slab", "scan"), None)),
        check_vma=False,
    )
```
